128 devices in a mesh: blk: 32 (over z, x_lo, y), grp: 4 (over x_hi, core).
Axes of the slice: x: 4 (x_hi: 2, x_lo: 2; x = x_hi * 2 + x_lo), y: 4, z: 4, core: 2. Of those that a mesh axis runs over, the one named last changes fastest.
Arguments:
- acts: bfloat16 [1, 512, 256, 4096], P(None, 'blk', 'grp'), may hold values from -6 to 6
- out_grads: bfloat16 [1, 512, 256, 4096], P(None, 'blk', 'grp'), may hold values from -6 to 6
- proj_in: bfloat16 [1, 4096, 64], replicated, may hold values from -0.09375 to 0.09375
- proj_out: bfloat16 [1, 4096, 64], replicated, may hold values from -0.09375 to 0.09375
- lengths: int32 [512], P('blk'), may hold values from 1 to 256
- queries: bfloat16 [2048, 4096], P('blk'), may hold values from -0.09375 to 0.09375
Outputs:
- scores: float32 [512, 2048], P(('blk', 'grp'))
The draws below stay inside these ranges and needn't reach their ends.
All inputs are finite; a program needn't handle non-finite values.
Results may differ from the reference program's by a relative error of at most 0.0049.
Values may be sent and summed in bfloat16 or wider, within the bound.
A program may use at most 128 MiB of HBM per device.

```python
import jax
import jax.numpy as jnp
from jax import lax

D = 4096
PR = 64
LAYERS = 1
SEQ = 256
PDIM = 4096
CAND = 512
QUERIES = 2048


def with_ends(values, key, least, largest):
    index_at = [jax.random.randint(jax.random.fold_in(key, axis), (), 0, length) for axis, length in enumerate(values.shape)]
    main_axis = values.shape.index(max(values.shape))
    next_to = index_at[:main_axis] + [(index_at[main_axis] + 1) % values.shape[main_axis]] + index_at[main_axis + 1:]
    return values.at[tuple(index_at)].set(least).at[tuple(next_to)].set(largest)


def levels(key, dims, cuts, least, high):
    level, own = 1.0, jax.random.fold_in(key, 6)
    for position, parts in cuts:
        draws = jnp.exp(jax.random.uniform(jax.random.fold_in(own, position), (parts,), jnp.float32, least / len(cuts), high / len(cuts)))
        level = level * jnp.repeat(draws, dims[position] // parts).reshape([-1 if axis == position else 1 for axis in range(len(dims))])
    return level


def bell_draw(own_key, dims, width, bound, shards=(), held_as=jnp.bfloat16):
    array = jax.random.normal(own_key, dims, jnp.float32) * width
    if len(shards) > 0:
        array = levels(own_key, dims, shards, -0.22, 0.18) * array
    return jnp.clip(array, min=-bound, max=bound).astype(held_as)


def setup_inputs(seed: int = 0) -> dict:
    keys = jax.random.split(jax.random.key(seed), 7)
    return {
        "acts": bell_draw(keys[0], (LAYERS, CAND, SEQ, D), 1.0, 6.0, ((1, 32), (2, 4))),
        "out_grads": bell_draw(keys[1], (LAYERS, CAND, SEQ, D), 1.0, 6.0, ((1, 32), (2, 4))),
        "proj_in": bell_draw(keys[2], (LAYERS, D, PR), D ** -0.5, 0.09375),
        "proj_out": bell_draw(keys[3], (LAYERS, D, PR), D ** -0.5, 0.09375),
        "lengths": with_ends(jax.random.randint(keys[4], (CAND,), 1, SEQ + 1), jax.random.fold_in(keys[4], 1), 1, SEQ).astype(jnp.int32),
        "queries": bell_draw(keys[5], (QUERIES, PDIM), PDIM ** -0.5, 0.09375, ((0, 32),)),
    }


def reference(acts, out_grads, proj_in, proj_out, lengths, queries):
    positions = jnp.arange(SEQ, dtype=jnp.int32)
    masked = (positions[None, :] < lengths[:, None]).astype(jnp.float32)
    blocks = []
    for layer in range(LAYERS):
        xp = jnp.dot(acts[layer].reshape(CAND * SEQ, D), proj_in[layer], preferred_element_type=jnp.float32)
        xp = xp.astype(jnp.bfloat16).reshape(CAND, SEQ, PR)
        gp = jnp.dot(out_grads[layer].reshape(CAND * SEQ, D), proj_out[layer], preferred_element_type=jnp.float32)
        gp = gp.astype(jnp.bfloat16).reshape(CAND, SEQ, PR)
        gmask = gp.astype(jnp.float32) * masked[:, :, None]
        block = jnp.einsum('cta,ctb->cab', gmask, xp.astype(jnp.float32))
        blocks.append(block.reshape(CAND, PR * PR))
    grads = jnp.concatenate(blocks, axis=1)
    scale = lax.rsqrt(lax.optimization_barrier(jnp.mean(grads * grads, axis=1, keepdims=True)) + 1e-06)
    unit = (grads * scale).astype(jnp.bfloat16)
    return jnp.dot(unit, queries.T, preferred_element_type=jnp.float32)
```

```python
import functools

import jax
import jax.numpy as jnp
from jax import lax
from jax.experimental import pallas as pl
from jax.experimental.pallas import tpu as pltpu
from jax.sharding import PartitionSpec as P

MESH = pl.DeviceIdType.MESH
BF16, F32 = jnp.bfloat16, jnp.float32
D, PR, TOK = 4096, 64, 64
NT = (((1,), (1,)), ((), ()))
TN = (((0,), (0,)), ((), ()))
CHUNKS, AHEAD = 8, 2


def kernel(lens, acts, og, wi, wo, q, out,
           abuf, gbuf, wib, wob, pscr, pown, psend, pbuf, usend, ubuf, uf, qbuf, ssend, sbuf,
           ld_sem, w_sem, q_ssem, q_rsem, c_ssem, c_rsem, e_ssem, e_rsem, s_ssem, s_rsem):
    b, g = lax.axis_index("blk"), lax.axis_index("grp")
    z, xl, y = b // 8, (b // 4) % 2, b % 4
    xh, core = g // 2, g % 2

    def dev(z_, xl_, y_, xh_, c_):
        return (z_ * 8 + xl_ * 4 + y_, xh_ * 2 + c_)

    up, down = (y + 1) % 4, (y + 3) % 4
    y_up, y_down = dev(z, xl, up, xh, core), dev(z, xl, down, xh, core)
    x_up = dev(z, 1 - xl, y, (xh + xl) % 2, core)
    x_down = dev(z, 1 - xl, y, (xh + 1 - xl) % 2, core)
    z_peers = [((z + dz) % 4, (core + dc) % 2) for dz, dc in
               ((2, 0), (2, 1), (1, 0), (3, 0), (1, 1), (3, 1), (0, 1))]

    def target(s):
        return (xh + 1 - s // 2) % 2, (core + (s + 1) // 2) % 2

    barrier = pltpu.get_barrier_semaphore()
    partners = [y_up, y_down, x_up, x_down]
    partners += [dev(z_, xl, y, xh, c_) for z_, c_ in z_peers]
    partners += [dev(z, xl, y, *target(s)) for s in range(2)]
    for p in partners:
        pl.semaphore_signal(barrier, inc=1, device_id=p, device_id_type=MESH)

    def load(k):
        xt, ct = target(k // 2)
        first = (xt * 2 + ct) * 4 + (k % 2) * 2
        src = pl.ds(first, 2)
        return (pltpu.make_async_copy(acts.at[src], abuf.at[pl.ds(2 * k, 2)], ld_sem.at[k, 0]),
                pltpu.make_async_copy(og.at[src], gbuf.at[pl.ds(2 * k, 2)], ld_sem.at[k, 1]))

    own = xl * 4 + y
    w_loads = [pltpu.make_async_copy(wi, wib, w_sem.at[0]),
               pltpu.make_async_copy(wo, wob, w_sem.at[1])]
    q_load = pltpu.make_async_copy(
        q.at[:, pl.ds(pl.multiple_of(core * 2048, 2048), 2048)], qbuf.at[own], w_sem.at[2])
    for c in w_loads:
        c.start()
    for k in range(AHEAD):
        for c in load(k):
            c.start()
    q_load.start()

    def piece(slot, h):
        return qbuf.at[slot, pl.ds(h * 32, 32)]

    q_sends = []

    def send_q(slot, h, to):
        c = pltpu.make_async_remote_copy(
            src_ref=piece(slot, h), dst_ref=piece(slot, h), send_sem=q_ssem.at[len(q_sends)],
            recv_sem=q_rsem.at[slot, h], device_id=to, device_id_type=MESH)
        c.start()
        q_sends.append((slot, h, to))

    def wait_q(slot, h):
        pltpu.make_async_remote_copy(
            src_ref=piece(slot, h), dst_ref=piece(slot, h), send_sem=q_ssem.at[0],
            recv_sem=q_rsem.at[slot, h], device_id=y_up, device_id_type=MESH).wait_recv()

    near_up, near_down, far = xl * 4 + up, xl * 4 + down, xl * 4 + (y + 2) % 4
    q_load.wait()
    pl.semaphore_wait(barrier, len(partners))
    send_q(own, 0, y_up)
    send_q(own, 1, y_down)
    send_q(own, 0, x_up)
    send_q(own, 1, x_down)
    send_q(own, 1, y_up)
    send_q(own, 0, y_down)

    for c in w_loads:
        c.wait()
    pos = lax.broadcasted_iota(jnp.int32, (TOK, PR), 0) + g * TOK

    def chunk(k):
        for c in load(k):
            c.wait()

        @pl.when(k + AHEAD < CHUNKS)
        def _():
            for c in load(k + AHEAD):
                c.start()

        s = k // 2
        xt, ct = target(s)
        first = (xt * 2 + ct) * 4 + (k % 2) * 2
        x = abuf[pl.ds(2 * k, 2)].reshape(2 * TOK, D)
        gr = gbuf[pl.ds(2 * k, 2)].reshape(2 * TOK, D)
        xp = lax.dot_general(x, wib[...], NT, preferred_element_type=F32).astype(BF16)
        gp = lax.dot_general(gr, wob[...], NT, preferred_element_type=F32)
        for i in range(2):
            rows = slice(i * TOK, (i + 1) * TOK)
            masked = jnp.where(pos < lens[first + i], gp[rows], 0.0).astype(BF16)
            pscr[i] = lax.dot_general(masked, xp[rows], TN, preferred_element_type=F32)
            part = jnp.concatenate(
                [pscr[i, pl.ds(0, 32, stride=2), :], pscr[i, pl.ds(1, 32, stride=2), :]], axis=1)
            pown[(k % 2) * 2 + i] = part
            psend[s, (k % 2) * 2 + i] = part.astype(BF16)

    def send_part(s):
        return pltpu.make_async_remote_copy(
            src_ref=psend.at[s], dst_ref=pbuf.at[g], send_sem=c_ssem.at[s], recv_sem=c_rsem.at[g],
            device_id=dev(z, xl, y, *target(s)), device_id_type=MESH)

    def run(first, last):
        def body(k, carry):
            chunk(k)
            return carry
        lax.fori_loop(first, last, body, 0)

    run(0, 2)
    send_part(0).start()
    run(2, 4)
    send_part(1).start()
    wait_q(near_down, 0)
    send_q(near_down, 0, y_up)
    send_q(near_down, 0, x_up)
    wait_q(near_up, 1)
    send_q(near_up, 1, y_down)
    send_q(near_up, 1, x_down)
    run(4, 6)
    send_part(2).start()
    wait_q(near_down, 1)
    send_q(near_down, 1, x_down)
    wait_q(near_up, 0)
    send_q(near_up, 0, x_up)
    run(6, 8)
    wait_q(far, 0)
    send_q(far, 0, x_up)
    wait_q(far, 1)
    send_q(far, 1, x_down)

    total = pown[...]
    for s in range(3):
        xt, ct = target(s)
        src = xt * 2 + ct
        pltpu.make_async_remote_copy(
            src_ref=psend.at[s], dst_ref=pbuf.at[src], send_sem=c_ssem.at[s],
            recv_sem=c_rsem.at[src], device_id=dev(z, xl, y, xt, ct), device_id_type=MESH).wait_recv()
        total = total + pbuf[src].astype(F32)
    square = jnp.sum(jnp.sum(total * total, axis=2, keepdims=True), axis=1, keepdims=True)
    unit = (total * lax.rsqrt(square * (1.0 / 4096) + 1e-6)).astype(BF16)
    usend[0] = unit[:, :16]
    usend[1] = unit[:, 16:]

    me = z * 2 + core

    def send_u(i):
        z_, c_ = z_peers[i]
        return pltpu.make_async_remote_copy(
            src_ref=usend.at[c_], dst_ref=ubuf.at[me], send_sem=e_ssem.at[i], recv_sem=e_rsem.at[me],
            device_id=dev(z_, xl, y, xh, c_), device_id_type=MESH)

    for i in range(7):
        send_u(i).start()
    ubuf[me] = usend[core]

    for slot_y in range(4):
        for h in range(2):
            wait_q((1 - xl) * 4 + slot_y, h)
    for z_, c_ in z_peers:
        o = z_ * 2 + c_
        pltpu.make_async_remote_copy(
            src_ref=usend.at[0], dst_ref=ubuf.at[o], send_sem=e_ssem.at[0], recv_sem=e_rsem.at[o],
            device_id=dev(z_, xl, y, xh, c_), device_id_type=MESH).wait_recv()
    uf[...] = ubuf[...].astype(F32).reshape(512, 128)
    left = jnp.concatenate(
        [uf[pl.ds(r, 32, stride=16), :].astype(BF16) for r in range(16)], axis=1)
    scores = lax.dot_general(left, qbuf[...].reshape(512, 2048), NT, preferred_element_type=F32)
    for o in range(8):
        ssend[o] = scores[4 * o:4 * o + 4]

    def send_s(i):
        z_, c_ = z_peers[i]
        return pltpu.make_async_remote_copy(
            src_ref=ssend.at[z_ * 2 + c_], dst_ref=sbuf.at[me], send_sem=s_ssem.at[i],
            recv_sem=s_rsem.at[me], device_id=dev(z_, xl, y, xh, c_), device_id_type=MESH)

    for i in range(7):
        send_s(i).start()
    sbuf[me] = ssend[me]
    for i in range(3):
        send_part(i).wait_send()
    for i, (slot, h, to) in enumerate(q_sends):
        pltpu.make_async_remote_copy(
            src_ref=piece(slot, h), dst_ref=piece(slot, h), send_sem=q_ssem.at[i],
            recv_sem=q_rsem.at[slot, h], device_id=to, device_id_type=MESH).wait_send()
    for i in range(7):
        send_u(i).wait_send()
    for z_, c_ in z_peers:
        o = z_ * 2 + c_
        pltpu.make_async_remote_copy(
            src_ref=ssend.at[0], dst_ref=sbuf.at[o], send_sem=s_ssem.at[0], recv_sem=s_rsem.at[o],
            device_id=dev(z_, xl, y, xh, c_), device_id_type=MESH).wait_recv()
    for z_ in range(4):
        out[:, z_ * 512:(z_ + 1) * 512] = sbuf[2 * z_] + sbuf[2 * z_ + 1]
    for i in range(7):
        send_s(i).wait_send()


def on_device(acts, out_grads, proj_in, proj_out, lengths, queries):
    any_space = pl.BlockSpec(memory_space=pltpu.HBM)
    dma = pltpu.SemaphoreType.DMA
    return pl.pallas_call(
        kernel,
        name="scores",
        out_shape=jax.ShapeDtypeStruct((4, 2048), F32),
        in_specs=[pl.BlockSpec(memory_space=pltpu.SMEM)] + [any_space] * 5,
        out_specs=pl.BlockSpec(memory_space=pltpu.VMEM),
        scratch_shapes=[
            pltpu.VMEM((16, TOK, D), BF16),
            pltpu.VMEM((16, TOK, D), BF16),
            pltpu.VMEM((PR, D), BF16),
            pltpu.VMEM((PR, D), BF16),
            pltpu.VMEM((2, PR, PR), F32),
            pltpu.VMEM((4, 32, 128), F32),
            pltpu.VMEM((4, 4, 32, 128), BF16),
            pltpu.VMEM((4, 4, 32, 128), BF16),
            pltpu.VMEM((2, 4, 16, 128), BF16),
            pltpu.VMEM((8, 4, 16, 128), BF16),
            pltpu.VMEM((512, 128), F32),
            pltpu.VMEM((8, 64, 2048), BF16),
            pltpu.VMEM((8, 4, 512), F32),
            pltpu.VMEM((8, 4, 512), F32),
            dma((CHUNKS, 2)), dma((3,)), dma((14,)), dma((8, 2)), dma((3,)), dma((4,)),
            dma((7,)), dma((8,)), dma((7,)), dma((8,)),
        ],
        compiler_params=pltpu.CompilerParams(
            collective_id=0, has_side_effects=True, vmem_limit_bytes=62 * 2**20),
    )(lengths, acts[0], out_grads[0], proj_in[0].T, proj_out[0].T, queries)


def solution(mesh):
    in_specs = (
        P(None, "blk", "grp", None),
        P(None, "blk", "grp", None),
        P(),
        P(),
        P("blk"),
        P("blk", None),
    )
    return jax.shard_map(
        on_device, mesh=mesh, in_specs=in_specs, out_specs=P(("blk", "grp"), None), check_vma=False
    )
```

```python
import functools

import jax
import jax.numpy as jnp
from jax import lax
from jax.experimental import pallas as pl
from jax.experimental.pallas import tpu as pltpu
from jax.sharding import PartitionSpec as P

MESH = pl.DeviceIdType.MESH
BF16, F32 = jnp.bfloat16, jnp.float32
D, PR, TOK = 4096, 64, 64
NT = (((1,), (1,)), ((), ()))
TN = (((0,), (0,)), ((), ()))
CHUNKS, AHEAD = 8, 2


def kernel(lens, acts, og, wi, wo, q, out,
           abuf, gbuf, wib, wob, pscr, pown, psend, pbuf, usend, ubuf, uf, qbuf, ssend, sbuf,
           ld_sem, w_sem, q_ssem, q_rsem, c_ssem, c_rsem, e_ssem, e_rsem, s_ssem, s_rsem):
    b, g = lax.axis_index("blk"), lax.axis_index("grp")
    z, xl, y = b // 8, (b // 4) % 2, b % 4
    xh, core = g // 2, g % 2

    def dev(z_, xl_, y_, xh_, c_):
        return (z_ * 8 + xl_ * 4 + y_, xh_ * 2 + c_)

    y_peers = [dev(z, xl, (y + dy) % 4, xh, core) for dy in (2, 1, 3)]
    peers = [((z + dz) % 4, (xl + dx) % 2, (core + dc) % 2)
             for dz in (2, 1, 3, 0) for dx in (1, 0) for dc in (0, 1) if (dz, dx, dc) != (0, 0, 0)]

    def peer(i):
        z_, xl_, c_ = peers[i]
        return dev(z_, xl_, y, xh, c_), (z_ * 2 + xl_) * 2 + c_

    def target(s):
        return (xh + 1 - s // 2) % 2, (core + (s + 1) // 2) % 2

    barrier = pltpu.get_barrier_semaphore()
    partners = y_peers + [peer(i)[0] for i in range(15)]
    partners += [dev(z, xl, y, *target(s)) for s in range(2)]
    for p in partners:
        pl.semaphore_signal(barrier, inc=1, device_id=p, device_id_type=MESH)

    def load(k):
        xt, ct = target(k // 2)
        first = (xt * 2 + ct) * 4 + (k % 2) * 2
        src = pl.ds(first, 2)
        return (pltpu.make_async_copy(acts.at[src], abuf.at[pl.ds(2 * k, 2)], ld_sem.at[k, 0]),
                pltpu.make_async_copy(og.at[src], gbuf.at[pl.ds(2 * k, 2)], ld_sem.at[k, 1]))

    w_loads = [pltpu.make_async_copy(wi, wib, w_sem.at[0]),
               pltpu.make_async_copy(wo, wob, w_sem.at[1])]
    q_load = pltpu.make_async_copy(
        q.at[:, pl.ds(pl.multiple_of(core * 2048, 2048), 2048)], qbuf.at[y], w_sem.at[2])
    for c in w_loads:
        c.start(priority=1)
    for k in range(AHEAD):
        for c in load(k):
            c.start(priority=1)
    q_load.start(priority=1)

    def send_q(i):
        return pltpu.make_async_remote_copy(
            src_ref=qbuf.at[y], dst_ref=qbuf.at[y], send_sem=q_ssem.at[i], recv_sem=q_rsem.at[y],
            device_id=y_peers[i], device_id_type=MESH)

    for c in w_loads:
        c.wait()
    pos = lax.broadcasted_iota(jnp.int32, (TOK, PR), 0) + g * TOK

    def chunk(k):
        for c in load(k):
            c.wait()

        @pl.when(k + AHEAD < CHUNKS)
        def _():
            for c in load(k + AHEAD):
                c.start(priority=1)

        s = k // 2
        xt, ct = target(s)
        first = (xt * 2 + ct) * 4 + (k % 2) * 2
        x = abuf[pl.ds(2 * k, 2)].reshape(2 * TOK, D)
        gr = gbuf[pl.ds(2 * k, 2)].reshape(2 * TOK, D)
        xp = lax.dot_general(x, wib[...], NT, preferred_element_type=F32).astype(BF16)
        gp = lax.dot_general(gr, wob[...], NT, preferred_element_type=F32)
        for i in range(2):
            rows = slice(i * TOK, (i + 1) * TOK)
            masked = jnp.where(pos < lens[first + i], gp[rows], 0.0).astype(BF16)
            pscr[i] = lax.dot_general(masked, xp[rows], TN, preferred_element_type=F32)
            part = jnp.concatenate(
                [pscr[i, pl.ds(0, 32, stride=2), :], pscr[i, pl.ds(1, 32, stride=2), :]], axis=1)
            pown[(k % 2) * 2 + i] = part
            psend[s, (k % 2) * 2 + i] = part.astype(BF16)

    def send_part(s):
        return pltpu.make_async_remote_copy(
            src_ref=psend.at[s], dst_ref=pbuf.at[g], send_sem=c_ssem.at[s], recv_sem=c_rsem.at[g],
            device_id=dev(z, xl, y, *target(s)), device_id_type=MESH)

    def run(first, last):
        def body(k, carry):
            chunk(k)
            return carry
        lax.fori_loop(first, last, body, 0)

    run(0, 1)
    q_load.wait()
    pl.semaphore_wait(barrier, len(partners))
    for i in range(3):
        send_q(i).start()
    run(1, 2)
    send_part(0).start()
    run(2, 4)
    send_part(1).start()
    run(4, 6)
    send_part(2).start()
    run(6, 8)

    total = pown[...]
    for s in range(3):
        xt, ct = target(s)
        src = xt * 2 + ct
        pltpu.make_async_remote_copy(
            src_ref=psend.at[s], dst_ref=pbuf.at[src], send_sem=c_ssem.at[s],
            recv_sem=c_rsem.at[src], device_id=dev(z, xl, y, xt, ct), device_id_type=MESH).wait_recv()
        total = total + pbuf[src].astype(F32)
    square = jnp.sum(jnp.sum(total * total, axis=2, keepdims=True), axis=1, keepdims=True)
    unit = (total * lax.rsqrt(square * (1.0 / 4096) + 1e-6)).astype(BF16)
    usend[0] = unit[:, :16]
    usend[1] = unit[:, 16:]

    me = (z * 2 + xl) * 2 + core

    def send_u(i):
        return pltpu.make_async_remote_copy(
            src_ref=usend.at[peers[i][2]], dst_ref=ubuf.at[me], send_sem=e_ssem.at[i],
            recv_sem=e_rsem.at[me], device_id=peer(i)[0], device_id_type=MESH)

    for i in range(15):
        send_u(i).start()
    ubuf[me] = usend[core]

    for i, dy in enumerate((2, 1, 3)):
        slot = (y + dy) % 4
        pltpu.make_async_remote_copy(
            src_ref=qbuf.at[slot], dst_ref=qbuf.at[slot], send_sem=q_ssem.at[i],
            recv_sem=q_rsem.at[slot], device_id=y_peers[i], device_id_type=MESH).wait_recv()
    for i in range(15):
        to, o = peer(i)
        pltpu.make_async_remote_copy(
            src_ref=usend.at[0], dst_ref=ubuf.at[o], send_sem=e_ssem.at[i], recv_sem=e_rsem.at[o],
            device_id=to, device_id_type=MESH).wait_recv()
    uf[...] = ubuf[...].astype(F32).reshape(1024, 128)
    left = jnp.concatenate(
        [uf[pl.ds(r, 64, stride=16), :].astype(BF16) for r in range(16)], axis=1)
    scores = lax.dot_general(left, qbuf[...].reshape(256, 2048), NT, preferred_element_type=F32)
    for o in range(16):
        ssend[o] = scores[4 * o:4 * o + 4]

    def send_s(i):
        to, o = peer(i)
        return pltpu.make_async_remote_copy(
            src_ref=ssend.at[o], dst_ref=sbuf.at[me], send_sem=s_ssem.at[i],
            recv_sem=s_rsem.at[me], device_id=to, device_id_type=MESH)

    for i in range(15):
        send_s(i).start()
    sbuf[me] = ssend[me]
    for i in range(3):
        send_part(i).wait_send()
        send_q(i).wait_send()
    for i in range(15):
        send_u(i).wait_send()
    for i in range(15):
        to, o = peer(i)
        pltpu.make_async_remote_copy(
            src_ref=ssend.at[0], dst_ref=sbuf.at[o], send_sem=s_ssem.at[i], recv_sem=s_rsem.at[o],
            device_id=to, device_id_type=MESH).wait_recv()
    for o in range(8):
        out[:, o * 256:(o + 1) * 256] = sbuf[2 * o] + sbuf[2 * o + 1]
    for i in range(15):
        send_s(i).wait_send()


def on_device(acts, out_grads, proj_in, proj_out, lengths, queries):
    any_space = pl.BlockSpec(memory_space=pltpu.HBM)
    dma = pltpu.SemaphoreType.DMA
    return pl.pallas_call(
        kernel,
        name="scores",
        out_shape=jax.ShapeDtypeStruct((4, 2048), F32),
        in_specs=[pl.BlockSpec(memory_space=pltpu.SMEM)] + [any_space] * 5,
        out_specs=pl.BlockSpec(memory_space=pltpu.VMEM),
        scratch_shapes=[
            pltpu.VMEM((16, TOK, D), BF16),
            pltpu.VMEM((16, TOK, D), BF16),
            pltpu.VMEM((PR, D), BF16),
            pltpu.VMEM((PR, D), BF16),
            pltpu.VMEM((2, PR, PR), F32),
            pltpu.VMEM((4, 32, 128), F32),
            pltpu.VMEM((4, 4, 32, 128), BF16),
            pltpu.VMEM((4, 4, 32, 128), BF16),
            pltpu.VMEM((2, 4, 16, 128), BF16),
            pltpu.VMEM((16, 4, 16, 128), BF16),
            pltpu.VMEM((1024, 128), F32),
            pltpu.VMEM((4, 64, 2048), BF16),
            pltpu.VMEM((16, 4, 256), F32),
            pltpu.VMEM((16, 4, 256), F32),
            dma((CHUNKS, 2)), dma((3,)), dma((3,)), dma((4,)), dma((3,)), dma((4,)),
            dma((15,)), dma((16,)), dma((15,)), dma((16,)),
        ],
        compiler_params=pltpu.CompilerParams(
            collective_id=0, has_side_effects=True, vmem_limit_bytes=62 * 2**20),
    )(lengths, acts[0], out_grads[0], proj_in[0].T, proj_out[0].T, queries)


def solution(mesh):
    in_specs = (
        P(None, "blk", "grp", None),
        P(None, "blk", "grp", None),
        P(),
        P(),
        P("blk"),
        P("blk", None),
    )
    return jax.shard_map(
        on_device, mesh=mesh, in_specs=in_specs, out_specs=P(("blk", "grp"), None), check_vma=False
    )
```

```python
import functools

import jax
import jax.numpy as jnp
from jax import lax
from jax.experimental import pallas as pl
from jax.experimental.pallas import tpu as pltpu
from jax.sharding import PartitionSpec as P

MESH = pl.DeviceIdType.MESH
BF16, F32 = jnp.bfloat16, jnp.float32
D, PR, TOK = 4096, 64, 64
NT = (((1,), (1,)), ((), ()))
TN = (((0,), (0,)), ((), ()))
COLS, AHEAD = 2048, 2
SPLIT = D // COLS
PIECES = 4 * SPLIT
FORWARD = 6


def kernel(lens_hbm, acts, og, wi, wo, q, out,
           abuf, gbuf, wib, wob, xacc, gacc, pscr, pown, psend, pbuf, usend, ubuf, uf, qbuf, ssend, sbuf,
           lens, ld_sem, w_sem, q_ssem, q_rsem, c_ssem, c_rsem, e_ssem, e_rsem, s_ssem, s_rsem):
    b, g = lax.axis_index("blk"), lax.axis_index("grp")
    z, xl, y = b // 8, (b // 4) % 2, b % 4
    xh, core = g // 2, g % 2

    def dev(z_, xl_, y_, xh_, c_):
        return (z_ * 8 + xl_ * 4 + y_, xh_ * 2 + c_)

    up, down, far = (y + 1) % 4, (y + 3) % 4, (y + 2) % 4
    y_up, y_down = dev(z, xl, up, xh, core), dev(z, xl, down, xh, core)
    peers = [((z + dz) % 4, (xl + dx) % 2, (core + dc) % 2)
             for dz in (2, 1, 3, 0) for dx in (1, 0) for dc in (0, 1) if (dz, dx, dc) != (0, 0, 0)]

    def peer(i):
        z_, xl_, c_ = peers[i]
        return dev(z_, xl_, y, xh, c_), (z_ * 2 + xl_) * 2 + c_

    def target(s):
        return (xh + 1 - s // 2) % 2, (core + (s + 1) // 2) % 2

    barrier = pltpu.get_barrier_semaphore()
    partners = [y_up, y_down] + [peer(i)[0] for i in range(15)]
    partners += [dev(z, xl, y, *target(s)) for s in range(2)]
    for p in partners:
        pl.semaphore_signal(barrier, inc=1, device_id=p, device_id_type=MESH)

    def load(i):
        xt, ct = target(i // SPLIT)
        rows = pl.ds((xt * 2 + ct) * 4, 4)
        cols = pl.ds(pl.multiple_of((i % SPLIT) * COLS, COLS), COLS)
        return (pltpu.make_async_copy(acts.at[rows, :, cols], abuf.at[i], ld_sem.at[i, 0]),
                pltpu.make_async_copy(og.at[rows, :, cols], gbuf.at[i], ld_sem.at[i, 1]))

    w_loads = [pltpu.make_async_copy(wi, wib.at[pl.ds(0, PR)], w_sem.at[0]),
               pltpu.make_async_copy(wo, wob, w_sem.at[1])]
    q_load = pltpu.make_async_copy(
        q.at[:, pl.ds(pl.multiple_of(core * 2048, 2048), 2048)], qbuf.at[y], w_sem.at[2])
    for c in w_loads:
        c.start(priority=1)
    for k in range(AHEAD):
        for c in load(k):
            c.start(priority=1)
    q_load.start(priority=1)
    l_load = pltpu.make_async_copy(lens_hbm, lens, w_sem.at[3])
    l_load.start()

    q_moves = [(y, 0, y_up), (y, 1, y_down), (y, 1, y_up), (y, 0, y_down), (down, 0, y_up), (up, 1, y_down)]

    def move_q(i):
        slot, h, to = q_moves[i]
        half = qbuf.at[slot, pl.ds(h * 32, 32)]
        return pltpu.make_async_remote_copy(
            src_ref=half, dst_ref=half, send_sem=q_ssem.at[i], recv_sem=q_rsem.at[slot, h],
            device_id=to, device_id_type=MESH)

    def wait_q(slot, h):
        half = qbuf.at[slot, pl.ds(h * 32, 32)]
        pltpu.make_async_remote_copy(
            src_ref=half, dst_ref=half, send_sem=q_ssem.at[0], recv_sem=q_rsem.at[slot, h],
            device_id=y_up, device_id_type=MESH).wait_recv()

    def send_part(s):
        return pltpu.make_async_remote_copy(
            src_ref=psend.at[s], dst_ref=pbuf.at[g], send_sem=c_ssem.at[s], recv_sem=c_rsem.at[g],
            device_id=dev(z, xl, y, *target(s)), device_id_type=MESH)

    for c in w_loads:
        c.wait()
    l_load.wait()
    wib[pl.ds(PR, PR)] = wib[pl.ds(0, PR)]
    pos = lax.broadcasted_iota(jnp.int32, (TOK, PR), 0) + g * TOK
    low = lax.broadcasted_iota(jnp.int32, (32, 128), 1) < PR

    def step(i, carry):
        s, k = i // SPLIT, i % SPLIT
        for c in load(i):
            c.wait()

        @pl.when(i + AHEAD < PIECES)
        def _():
            for c in load(i + AHEAD):
                c.start(priority=1)

        cols = pl.ds(pl.multiple_of(k * COLS, COLS), COLS)
        xp = lax.dot_general(
            abuf[i].reshape(4 * TOK, COLS), wib[:, cols], NT, preferred_element_type=F32)
        gp = lax.dot_general(
            gbuf[i].reshape(4 * TOK, COLS), wob[:, cols], NT, preferred_element_type=F32)

        @pl.when(k == 0)
        def _():
            xacc[...] = xp
            gacc[...] = gp

        @pl.when(k > 0)
        def _():
            xacc[...] += xp
            gacc[...] += gp

        @pl.when(i == 0)
        def _():
            q_load.wait()
            pl.semaphore_wait(barrier, len(partners))
            for j in range(4):
                move_q(j).start()

        @pl.when(k == SPLIT - 1)
        def _():
            xt, ct = target(s)
            for c in range(4):
                rows = pl.ds(c * TOK, TOK)
                left = jnp.where(pos < lens[(xt * 2 + ct) * 4 + c], gacc[rows], 0.0).astype(BF16)
                pscr[c] = lax.dot_general(
                    left, xacc[rows].astype(BF16), TN, preferred_element_type=F32)
                part = jnp.where(
                    low, pscr[c, pl.ds(0, 32, stride=2), :], pscr[c, pl.ds(1, 32, stride=2), :])
                pown[c] = part
                psend[s, c] = part.astype(BF16)

        @pl.when(jnp.logical_and(k == SPLIT - 1, s < 3))
        def _():
            send_part(s).start()

        @pl.when(i == FORWARD)
        def _():
            wait_q(down, 0)
            move_q(4).start()
            wait_q(up, 1)
            move_q(5).start()

        return carry

    lax.fori_loop(0, PIECES, step, 0)

    total = pown[...]
    for s in range(3):
        xt, ct = target(s)
        src = xt * 2 + ct
        pltpu.make_async_remote_copy(
            src_ref=psend.at[s], dst_ref=pbuf.at[src], send_sem=c_ssem.at[s],
            recv_sem=c_rsem.at[src], device_id=dev(z, xl, y, xt, ct), device_id_type=MESH).wait_recv()
        total = total + pbuf[src].astype(F32)
    square = jnp.sum(jnp.sum(total * total, axis=2, keepdims=True), axis=1, keepdims=True)
    unit = (total * lax.rsqrt(square * (1.0 / 4096) + 1e-6)).astype(BF16)
    usend[0] = unit[:, :16]
    usend[1] = unit[:, 16:]

    me = (z * 2 + xl) * 2 + core

    def send_u(i):
        return pltpu.make_async_remote_copy(
            src_ref=usend.at[peers[i][2]], dst_ref=ubuf.at[me], send_sem=e_ssem.at[i],
            recv_sem=e_rsem.at[me], device_id=peer(i)[0], device_id_type=MESH)

    for i in range(15):
        send_u(i).start()
    ubuf[me] = usend[core]

    for slot, h in ((down, 1), (up, 0), (far, 0), (far, 1)):
        wait_q(slot, h)
    for i in range(15):
        to, o = peer(i)
        pltpu.make_async_remote_copy(
            src_ref=usend.at[0], dst_ref=ubuf.at[o], send_sem=e_ssem.at[i], recv_sem=e_rsem.at[o],
            device_id=to, device_id_type=MESH).wait_recv()
    uf[...] = ubuf[...].astype(F32).reshape(1024, 128)
    left = jnp.concatenate(
        [uf[pl.ds(r, 64, stride=16), :].astype(BF16) for r in range(16)], axis=1)
    scores = lax.dot_general(left, qbuf[...].reshape(256, 2048), NT, preferred_element_type=F32)
    for o in range(16):
        ssend[o] = scores[4 * o:4 * o + 4]

    def send_s(i):
        to, o = peer(i)
        return pltpu.make_async_remote_copy(
            src_ref=ssend.at[o], dst_ref=sbuf.at[me], send_sem=s_ssem.at[i],
            recv_sem=s_rsem.at[me], device_id=to, device_id_type=MESH)

    for i in range(15):
        send_s(i).start()
    sbuf[me] = ssend[me]
    for i in range(3):
        send_part(i).wait_send()
    for i in range(6):
        move_q(i).wait_send()
    for i in range(15):
        send_u(i).wait_send()
    for i in range(15):
        to, o = peer(i)
        pltpu.make_async_remote_copy(
            src_ref=ssend.at[0], dst_ref=sbuf.at[o], send_sem=s_ssem.at[i], recv_sem=s_rsem.at[o],
            device_id=to, device_id_type=MESH).wait_recv()
    for o in range(8):
        out[:, o * 256:(o + 1) * 256] = sbuf[2 * o] + sbuf[2 * o + 1]
    for i in range(15):
        send_s(i).wait_send()


def on_device(acts, out_grads, proj_in, proj_out, lengths, queries):
    any_space = pl.BlockSpec(memory_space=pltpu.HBM)
    dma = pltpu.SemaphoreType.DMA
    return pl.pallas_call(
        kernel,
        name="scores",
        out_shape=pltpu.VMEM((4, 2048), F32),
        in_specs=[any_space] * 6,
        out_specs=pl.BlockSpec(memory_space=pltpu.VMEM),
        scratch_shapes=[
            pltpu.VMEM((PIECES, 4, TOK, COLS), BF16),
            pltpu.VMEM((PIECES, 4, TOK, COLS), BF16),
            pltpu.VMEM((2 * PR, D), BF16),
            pltpu.VMEM((PR, D), BF16),
            pltpu.VMEM((4 * TOK, 2 * PR), F32),
            pltpu.VMEM((4 * TOK, PR), F32),
            pltpu.VMEM((4, PR, 2 * PR), F32),
            pltpu.VMEM((4, 32, 128), F32),
            pltpu.VMEM((4, 4, 32, 128), BF16),
            pltpu.VMEM((4, 4, 32, 128), BF16),
            pltpu.VMEM((2, 4, 16, 128), BF16),
            pltpu.VMEM((16, 4, 16, 128), BF16),
            pltpu.VMEM((1024, 128), F32),
            pltpu.VMEM((4, 64, 2048), BF16),
            pltpu.VMEM((16, 4, 256), F32),
            pltpu.VMEM((16, 4, 256), F32),
            pltpu.SMEM((16,), jnp.int32), dma((PIECES, 2)), dma((4,)), dma((6,)), dma((4, 2)), dma((3,)), dma((4,)),
            dma((15,)), dma((16,)), dma((15,)), dma((16,)),
        ],
        compiler_params=pltpu.CompilerParams(
            collective_id=0, has_side_effects=True, vmem_limit_bytes=62*2**20),
    )(lengths, acts[0], out_grads[0], proj_in[0].T, proj_out[0].T, queries)


def solution(mesh):
    in_specs = (
        P(None, "blk", "grp", None),
        P(None, "blk", "grp", None),
        P(),
        P(),
        P("blk"),
        P("blk", None),
    )
    return jax.shard_map(
        on_device, mesh=mesh, in_specs=in_specs, out_specs=P(("blk", "grp"), None), check_vma=False
    )
```

```python
import functools

import jax
import jax.numpy as jnp
from jax import lax
from jax.experimental import pallas as pl
from jax.experimental.pallas import tpu as pltpu
from jax.sharding import PartitionSpec as P

MESH = pl.DeviceIdType.MESH
BF16, F32 = jnp.bfloat16, jnp.float32
D, PR, TOK = 4096, 64, 64
NT = (((1,), (1,)), ((), ()))
TN = (((0,), (0,)), ((), ()))
COLS, AHEAD = 2048, 2
SPLIT = D // COLS
PIECES = 4 * SPLIT
FORWARD = 6


def kernel(lens_hbm, acts, og, wi, wo, q, out,
           abuf, gbuf, wib, wob, xacc, gacc, pscr, pown, psend, pbuf, usend, ubuf, uf, qbuf, ssend, sbuf,
           lens, ld_sem, w_sem, q_ssem, q_rsem, c_ssem, c_rsem, e_ssem, e_rsem, s_ssem, s_rsem):
    b, g = lax.axis_index("blk"), lax.axis_index("grp")
    z, xl, y = b // 8, (b // 4) % 2, b % 4
    xh, core = g // 2, g % 2

    def dev(z_, xl_, y_, xh_, c_):
        return (z_ * 8 + xl_ * 4 + y_, xh_ * 2 + c_)

    up, down, far = (y + 1) % 4, (y + 3) % 4, (y + 2) % 4
    y_up, y_down = dev(z, xl, up, xh, core), dev(z, xl, down, xh, core)
    peers = [((z + dz) % 4, (xl + dx) % 2, (core + dc) % 2)
             for dz in (2, 1, 3, 0) for dx in (1, 0) for dc in (0, 1) if (dz, dx, dc) != (0, 0, 0)]

    def peer(i):
        z_, xl_, c_ = peers[i]
        return dev(z_, xl_, y, xh, c_), (z_ * 2 + xl_) * 2 + c_

    def target(s):
        return (xh + 1 - s // 2) % 2, (core + (s + 1) // 2) % 2

    barrier = pltpu.get_barrier_semaphore()
    partners = [y_up, y_down] + [peer(i)[0] for i in range(15)]
    partners += [dev(z, xl, y, *target(s)) for s in range(2)]

    def load(i):
        xt, ct = target(i // SPLIT)
        rows = pl.ds((xt * 2 + ct) * 4, 4)
        cols = pl.ds(pl.multiple_of((i % SPLIT) * COLS, COLS), COLS)
        return (pltpu.make_async_copy(acts.at[rows, :, cols], abuf.at[i], ld_sem.at[i, 0]),
                pltpu.make_async_copy(og.at[rows, :, cols], gbuf.at[i], ld_sem.at[i, 1]))

    w_loads = [pltpu.make_async_copy(wi, wib.at[pl.ds(0, PR)], w_sem.at[0]),
               pltpu.make_async_copy(wo, wob, w_sem.at[1])]
    q_load = pltpu.make_async_copy(
        q.at[:, pl.ds(pl.multiple_of(core * 2048, 2048), 2048)], qbuf.at[y], w_sem.at[2])
    for c in (*w_loads, *load(0)):
        c.start(priority=1)
    for p in partners:
        pl.semaphore_signal(barrier, inc=1, device_id=p, device_id_type=MESH)
    for c in (*load(1), q_load):
        c.start(priority=1)
    l_load = pltpu.make_async_copy(lens_hbm, lens, w_sem.at[3])
    l_load.start()

    q_moves = [(y, 0, y_up), (y, 1, y_down), (y, 1, y_up), (y, 0, y_down), (down, 0, y_up), (up, 1, y_down)]

    def move_q(i):
        slot, h, to = q_moves[i]
        half = qbuf.at[slot, pl.ds(h * 32, 32)]
        return pltpu.make_async_remote_copy(
            src_ref=half, dst_ref=half, send_sem=q_ssem.at[i], recv_sem=q_rsem.at[slot, h],
            device_id=to, device_id_type=MESH)

    def wait_q(slot, h):
        half = qbuf.at[slot, pl.ds(h * 32, 32)]
        pltpu.make_async_remote_copy(
            src_ref=half, dst_ref=half, send_sem=q_ssem.at[0], recv_sem=q_rsem.at[slot, h],
            device_id=y_up, device_id_type=MESH).wait_recv()

    def send_part(s):
        return pltpu.make_async_remote_copy(
            src_ref=psend.at[s], dst_ref=pbuf.at[g], send_sem=c_ssem.at[s], recv_sem=c_rsem.at[g],
            device_id=dev(z, xl, y, *target(s)), device_id_type=MESH)

    for c in w_loads:
        c.wait()
    l_load.wait()
    wib[pl.ds(PR, PR)] = wib[pl.ds(0, PR)]
    pos = lax.broadcasted_iota(jnp.int32, (TOK, PR), 0) + g * TOK
    low = lax.broadcasted_iota(jnp.int32, (32, 128), 1) < PR

    def step(i, carry):
        s, k = i // SPLIT, i % SPLIT
        for c in load(i):
            c.wait()

        @pl.when(i + AHEAD < PIECES)
        def _():
            for c in load(i + AHEAD):
                c.start(priority=1)

        cols = pl.ds(pl.multiple_of(k * COLS, COLS), COLS)
        xp = lax.dot_general(
            abuf[i].reshape(4 * TOK, COLS), wib[:, cols], NT, preferred_element_type=F32)
        gp = lax.dot_general(
            gbuf[i].reshape(4 * TOK, COLS), wob[:, cols], NT, preferred_element_type=F32)

        @pl.when(k == 0)
        def _():
            xacc[...] = xp
            gacc[...] = gp

        @pl.when(k > 0)
        def _():
            xacc[...] += xp
            gacc[...] += gp

        @pl.when(i == 0)
        def _():
            q_load.wait()
            pl.semaphore_wait(barrier, len(partners))
            for j in range(4):
                move_q(j).start()

        @pl.when(k == SPLIT - 1)
        def _():
            xt, ct = target(s)
            for c in range(4):
                rows = pl.ds(c * TOK, TOK)
                left = jnp.where(pos < lens[(xt * 2 + ct) * 4 + c], gacc[rows], 0.0).astype(BF16)
                pscr[c] = lax.dot_general(
                    left, xacc[rows].astype(BF16), TN, preferred_element_type=F32)
                part = jnp.where(
                    low, pscr[c, pl.ds(0, 32, stride=2), :], pscr[c, pl.ds(1, 32, stride=2), :])
                pown[c] = part
                psend[s, c] = part.astype(BF16)

        @pl.when(jnp.logical_and(k == SPLIT - 1, s < 3))
        def _():
            send_part(s).start()

        @pl.when(i == FORWARD)
        def _():
            wait_q(down, 0)
            move_q(4).start()
            wait_q(up, 1)
            move_q(5).start()

        return carry

    lax.fori_loop(0, PIECES, step, 0)

    total = pown[...]
    for s in range(3):
        xt, ct = target(s)
        src = xt * 2 + ct
        pltpu.make_async_remote_copy(
            src_ref=psend.at[s], dst_ref=pbuf.at[src], send_sem=c_ssem.at[s],
            recv_sem=c_rsem.at[src], device_id=dev(z, xl, y, xt, ct), device_id_type=MESH).wait_recv()
        total = total + pbuf[src].astype(F32)
    unit = total.astype(BF16)
    usend[0] = unit[:, :16]
    usend[1] = unit[:, 16:]

    me = (z * 2 + xl) * 2 + core

    def send_u(i):
        return pltpu.make_async_remote_copy(
            src_ref=usend.at[peers[i][2]], dst_ref=ubuf.at[me], send_sem=e_ssem.at[i],
            recv_sem=e_rsem.at[me], device_id=peer(i)[0], device_id_type=MESH)

    for i in range(15):
        send_u(i).start()
    ubuf[me] = usend[core]
    square = jnp.sum(jnp.sum(total * total, axis=2, keepdims=True), axis=1, keepdims=True)
    scale = lax.rsqrt(square * (1.0 / 4096) + 1e-6)[:, :, 0]

    for slot, h in ((down, 1), (up, 0), (far, 0), (far, 1)):
        wait_q(slot, h)
    def lay_out(o):
        uf[pl.ds(pl.multiple_of(o * 64, 64), 64)] = ubuf[o].astype(F32).reshape(64, 128)

    lay_out(me)
    for i in reversed(range(15)):
        to, o = peer(i)
        pltpu.make_async_remote_copy(
            src_ref=usend.at[0], dst_ref=ubuf.at[o], send_sem=e_ssem.at[i], recv_sem=e_rsem.at[o],
            device_id=to, device_id_type=MESH).wait_recv()
        lay_out(o)
    left = jnp.concatenate(
        [uf[pl.ds(r, 64, stride=16), :].astype(BF16) for r in range(16)], axis=1)
    scores = lax.dot_general(left, qbuf[...].reshape(256, 2048), NT, preferred_element_type=F32)
    for o in range(16):
        ssend[o] = scores[4 * o:4 * o + 4]

    def send_s(i):
        to, o = peer(i)
        return pltpu.make_async_remote_copy(
            src_ref=ssend.at[o], dst_ref=sbuf.at[me], send_sem=s_ssem.at[i],
            recv_sem=s_rsem.at[me], device_id=to, device_id_type=MESH)

    for i in range(15):
        send_s(i).start()
    sbuf[me] = ssend[me]
    for i in range(3):
        send_part(i).wait_send()
    for i in range(6):
        move_q(i).wait_send()
    for i in range(15):
        send_u(i).wait_send()
    for i in range(15):
        to, o = peer(i)
        pltpu.make_async_remote_copy(
            src_ref=ssend.at[0], dst_ref=sbuf.at[o], send_sem=s_ssem.at[i], recv_sem=s_rsem.at[o],
            device_id=to, device_id_type=MESH).wait_recv()
    for o in range(8):
        out[:, o * 256:(o + 1) * 256] = (sbuf[2 * o] + sbuf[2 * o + 1]) * scale
    for i in range(15):
        send_s(i).wait_send()


def on_device(acts, out_grads, proj_in, proj_out, lengths, queries):
    any_space = pl.BlockSpec(memory_space=pltpu.HBM)
    dma = pltpu.SemaphoreType.DMA
    return pl.pallas_call(
        kernel,
        name="scores",
        out_shape=pltpu.VMEM((4, 2048), F32),
        in_specs=[any_space] * 6,
        out_specs=pl.BlockSpec(memory_space=pltpu.VMEM),
        scratch_shapes=[
            pltpu.VMEM((PIECES, 4, TOK, COLS), BF16),
            pltpu.VMEM((PIECES, 4, TOK, COLS), BF16),
            pltpu.VMEM((2 * PR, D), BF16),
            pltpu.VMEM((PR, D), BF16),
            pltpu.VMEM((4 * TOK, 2 * PR), F32),
            pltpu.VMEM((4 * TOK, PR), F32),
            pltpu.VMEM((4, PR, 2 * PR), F32),
            pltpu.VMEM((4, 32, 128), F32),
            pltpu.VMEM((4, 4, 32, 128), BF16),
            pltpu.VMEM((4, 4, 32, 128), BF16),
            pltpu.VMEM((2, 4, 16, 128), BF16),
            pltpu.VMEM((16, 4, 16, 128), BF16),
            pltpu.VMEM((1024, 128), F32),
            pltpu.VMEM((4, 64, 2048), BF16),
            pltpu.VMEM((16, 4, 256), F32),
            pltpu.VMEM((16, 4, 256), F32),
            pltpu.SMEM((16,), jnp.int32), dma((PIECES, 2)), dma((4,)), dma((6,)), dma((4, 2)), dma((3,)), dma((4,)),
            dma((15,)), dma((16,)), dma((15,)), dma((16,)),
        ],
        compiler_params=pltpu.CompilerParams(
            collective_id=0, has_side_effects=True, vmem_limit_bytes=62*2**20),
    )(lengths, acts[0], out_grads[0], proj_in[0].T, proj_out[0].T, queries)


def solution(mesh):
    in_specs = (
        P(None, "blk", "grp", None),
        P(None, "blk", "grp", None),
        P(),
        P(),
        P("blk"),
        P("blk", None),
    )
    return jax.shard_map(
        on_device, mesh=mesh, in_specs=in_specs, out_specs=P(("blk", "grp"), None), check_vma=False
    )
```

```python
import functools

import jax
import jax.numpy as jnp
from jax import lax
from jax.experimental import pallas as pl
from jax.experimental.pallas import tpu as pltpu
from jax.sharding import PartitionSpec as P

MESH = pl.DeviceIdType.MESH
BF16, F32 = jnp.bfloat16, jnp.float32
D, PR, TOK = 4096, 64, 64
NT = (((1,), (1,)), ((), ()))
TN = (((0,), (0,)), ((), ()))
COLS, AHEAD = 2048, 2
SPLIT = D // COLS
PIECES = 4 * SPLIT
FORWARD = 6


def kernel(lens_hbm, acts, og, wi, wo, q, out,
           abuf, gbuf, wib, wob, xacc, gacc, pscr, pown, psend, pbuf, usend, ubuf, uf, qbuf, ssend, sbuf,
           lens, ld_sem, w_sem, q_ssem, q_rsem, c_ssem, c_rsem, e_ssem, e_rsem, s_ssem, s_rsem):
    b, g = lax.axis_index("blk"), lax.axis_index("grp")
    z, xl, y = b // 8, (b // 4) % 2, b % 4
    xh, core = g // 2, g % 2

    def dev(z_, xl_, y_, xh_, c_):
        return (z_ * 8 + xl_ * 4 + y_, xh_ * 2 + c_)

    up, down, far = (y + 1) % 4, (y + 3) % 4, (y + 2) % 4
    y_up, y_down = dev(z, xl, up, xh, core), dev(z, xl, down, xh, core)
    peers = [((z + dz) % 4, (xl + dx) % 2, (core + dc) % 2)
             for dz in (2, 1, 3, 0) for dx in (1, 0) for dc in (0, 1) if (dz, dx, dc) != (0, 0, 0)]

    def peer(i):
        z_, xl_, c_ = peers[i]
        return dev(z_, xl_, y, xh, c_), (z_ * 2 + xl_) * 2 + c_

    def target(s):
        return (xh + 1 - s // 2) % 2, (core + (s + 1) // 2) % 2

    barrier = pltpu.get_barrier_semaphore()
    partners = [y_up, y_down] + [peer(i)[0] for i in range(15)]
    partners += [dev(z, xl, y, *target(s)) for s in range(2)]
    for p in partners:
        pl.semaphore_signal(barrier, inc=1, device_id=p, device_id_type=MESH)

    def load(i):
        xt, ct = target(i // SPLIT)
        rows = pl.ds((xt * 2 + ct) * 4, 4)
        cols = pl.ds(pl.multiple_of((i % SPLIT) * COLS, COLS), COLS)
        return (pltpu.make_async_copy(acts.at[rows, :, cols], abuf.at[i], ld_sem.at[i, 0]),
                pltpu.make_async_copy(og.at[rows, :, cols], gbuf.at[i], ld_sem.at[i, 1]))

    w_loads = [pltpu.make_async_copy(wi, wib.at[pl.ds(0, PR)], w_sem.at[0]),
               pltpu.make_async_copy(wo, wob, w_sem.at[1])]
    q_load = pltpu.make_async_copy(
        q.at[:, pl.ds(pl.multiple_of(core * 2048, 2048), 2048)], qbuf.at[y], w_sem.at[2])
    for c in w_loads:
        c.start(priority=1)
    for k in range(AHEAD):
        for c in load(k):
            c.start(priority=1)
    q_load.start(priority=1)
    l_load = pltpu.make_async_copy(lens_hbm, lens, w_sem.at[3])
    l_load.start()

    q_moves = [(y, 0, y_up), (y, 1, y_down), (y, 1, y_up), (y, 0, y_down), (down, 0, y_up), (up, 1, y_down)]

    def move_q(i):
        slot, h, to = q_moves[i]
        half = qbuf.at[slot, pl.ds(h * 32, 32)]
        return pltpu.make_async_remote_copy(
            src_ref=half, dst_ref=half, send_sem=q_ssem.at[i], recv_sem=q_rsem.at[slot, h],
            device_id=to, device_id_type=MESH)

    def wait_q(slot, h):
        half = qbuf.at[slot, pl.ds(h * 32, 32)]
        pltpu.make_async_remote_copy(
            src_ref=half, dst_ref=half, send_sem=q_ssem.at[0], recv_sem=q_rsem.at[slot, h],
            device_id=y_up, device_id_type=MESH).wait_recv()

    def send_part(s):
        return pltpu.make_async_remote_copy(
            src_ref=psend.at[s], dst_ref=pbuf.at[g], send_sem=c_ssem.at[s], recv_sem=c_rsem.at[g],
            device_id=dev(z, xl, y, *target(s)), device_id_type=MESH)

    for c in w_loads:
        c.wait()
    l_load.wait()
    wib[pl.ds(PR, PR)] = wib[pl.ds(0, PR)]
    pos = lax.broadcasted_iota(jnp.int32, (TOK, PR), 0) + g * TOK
    low = lax.broadcasted_iota(jnp.int32, (32, 128), 1) < PR

    def step(i, carry):
        s, k = i // SPLIT, i % SPLIT
        for c in load(i):
            c.wait()

        @pl.when(i + AHEAD < PIECES)
        def _():
            for c in load(i + AHEAD):
                c.start(priority=1)

        cols = pl.ds(pl.multiple_of(k * COLS, COLS), COLS)
        xp = lax.dot_general(
            abuf[i].reshape(4 * TOK, COLS), wib[:, cols], NT, preferred_element_type=F32)
        gp = lax.dot_general(
            gbuf[i].reshape(4 * TOK, COLS), wob[:, cols], NT, preferred_element_type=F32)

        @pl.when(k == 0)
        def _():
            xacc[...] = xp
            gacc[...] = gp

        @pl.when(k > 0)
        def _():
            xacc[...] += xp
            gacc[...] += gp

        @pl.when(i == 0)
        def _():
            q_load.wait()
            pl.semaphore_wait(barrier, len(partners))
            for j in range(4):
                move_q(j).start()

        @pl.when(k == SPLIT - 1)
        def _():
            xt, ct = target(s)
            for c in range(4):
                rows = pl.ds(c * TOK, TOK)
                left = jnp.where(pos < lens[(xt * 2 + ct) * 4 + c], gacc[rows], 0.0).astype(BF16)
                pscr[c] = lax.dot_general(
                    left, xacc[rows].astype(BF16), TN, preferred_element_type=F32)
                part = jnp.where(
                    low, pscr[c, pl.ds(0, 32, stride=2), :], pscr[c, pl.ds(1, 32, stride=2), :])
                pown[c] = part
                psend[s, c] = part.astype(BF16)

        @pl.when(jnp.logical_and(k == SPLIT - 1, s < 3))
        def _():
            send_part(s).start()

        @pl.when(i == FORWARD)
        def _():
            wait_q(down, 0)
            move_q(4).start()
            wait_q(up, 1)
            move_q(5).start()

        return carry

    lax.fori_loop(0, PIECES, step, 0)

    total = pown[...]
    for s in range(3):
        xt, ct = target(s)
        src = xt * 2 + ct
        pltpu.make_async_remote_copy(
            src_ref=psend.at[s], dst_ref=pbuf.at[src], send_sem=c_ssem.at[s],
            recv_sem=c_rsem.at[src], device_id=dev(z, xl, y, xt, ct), device_id_type=MESH).wait_recv()
        total = total + pbuf[src].astype(F32)
    square = jnp.sum(jnp.sum(total * total, axis=2, keepdims=True), axis=1, keepdims=True)
    unit = (total * lax.rsqrt(square * (1.0 / 4096) + 1e-6)).astype(BF16)
    usend[0] = unit[:, :16]
    usend[1] = unit[:, 16:]

    me = (z * 2 + xl) * 2 + core

    def send_u(i):
        return pltpu.make_async_remote_copy(
            src_ref=usend.at[peers[i][2]], dst_ref=ubuf.at[me], send_sem=e_ssem.at[i],
            recv_sem=e_rsem.at[0], device_id=peer(i)[0], device_id_type=MESH)

    for i in range(15):
        send_u(i).start()
    ubuf[me] = usend[core]

    for slot, h in ((down, 1), (up, 0), (far, 0), (far, 1)):
        wait_q(slot, h)
    fifteen = pl.ds(0, 15)
    pltpu.make_async_remote_copy(
        src_ref=ubuf.at[fifteen], dst_ref=ubuf.at[fifteen], send_sem=e_ssem.at[0],
        recv_sem=e_rsem.at[0], device_id=peer(0)[0], device_id_type=MESH).wait_recv()
    uf[...] = ubuf[...].astype(F32).reshape(1024, 128)
    left = jnp.concatenate(
        [uf[pl.ds(r, 64, stride=16), :].astype(BF16) for r in range(16)], axis=1)
    scores = lax.dot_general(left, qbuf[...].reshape(256, 2048), NT, preferred_element_type=F32)
    for o in range(16):
        ssend[o] = scores[4 * o:4 * o + 4]

    def send_s(i):
        to, o = peer(i)
        return pltpu.make_async_remote_copy(
            src_ref=ssend.at[o], dst_ref=sbuf.at[me], send_sem=s_ssem.at[i],
            recv_sem=s_rsem.at[0], device_id=to, device_id_type=MESH)

    for i in range(15):
        send_s(i).start()
    sbuf[me] = ssend[me]
    for i in range(3):
        send_part(i).wait_send()
    for i in range(6):
        move_q(i).wait_send()
    for i in range(15):
        send_u(i).wait_send()
    pltpu.make_async_remote_copy(
        src_ref=sbuf.at[fifteen], dst_ref=sbuf.at[fifteen], send_sem=s_ssem.at[0],
        recv_sem=s_rsem.at[0], device_id=peer(0)[0], device_id_type=MESH).wait_recv()
    for o in range(8):
        out[:, o * 256:(o + 1) * 256] = sbuf[2 * o] + sbuf[2 * o + 1]
    for i in range(15):
        send_s(i).wait_send()


def on_device(acts, out_grads, proj_in, proj_out, lengths, queries):
    any_space = pl.BlockSpec(memory_space=pltpu.HBM)
    dma = pltpu.SemaphoreType.DMA
    return pl.pallas_call(
        kernel,
        name="scores",
        out_shape=pltpu.VMEM((4, 2048), F32),
        in_specs=[any_space] * 6,
        out_specs=pl.BlockSpec(memory_space=pltpu.VMEM),
        scratch_shapes=[
            pltpu.VMEM((PIECES, 4, TOK, COLS), BF16),
            pltpu.VMEM((PIECES, 4, TOK, COLS), BF16),
            pltpu.VMEM((2 * PR, D), BF16),
            pltpu.VMEM((PR, D), BF16),
            pltpu.VMEM((4 * TOK, 2 * PR), F32),
            pltpu.VMEM((4 * TOK, PR), F32),
            pltpu.VMEM((4, PR, 2 * PR), F32),
            pltpu.VMEM((4, 32, 128), F32),
            pltpu.VMEM((4, 4, 32, 128), BF16),
            pltpu.VMEM((4, 4, 32, 128), BF16),
            pltpu.VMEM((2, 4, 16, 128), BF16),
            pltpu.VMEM((16, 4, 16, 128), BF16),
            pltpu.VMEM((1024, 128), F32),
            pltpu.VMEM((4, 64, 2048), BF16),
            pltpu.VMEM((16, 4, 256), F32),
            pltpu.VMEM((16, 4, 256), F32),
            pltpu.SMEM((16,), jnp.int32), dma((PIECES, 2)), dma((4,)), dma((6,)), dma((4, 2)), dma((3,)), dma((4,)),
            dma((15,)), dma((1,)), dma((15,)), dma((1,)),
        ],
        compiler_params=pltpu.CompilerParams(
            collective_id=0, has_side_effects=True, vmem_limit_bytes=62*2**20),
    )(lengths, acts[0], out_grads[0], proj_in[0].T, proj_out[0].T, queries)


def solution(mesh):
    in_specs = (
        P(None, "blk", "grp", None),
        P(None, "blk", "grp", None),
        P(),
        P(),
        P("blk"),
        P("blk", None),
    )
    return jax.shard_map(
        on_device, mesh=mesh, in_specs=in_specs, out_specs=P(("blk", "grp"), None), check_vma=False
    )
```

```python
import functools

import jax
import jax.numpy as jnp
from jax import lax
from jax.experimental import pallas as pl
from jax.experimental.pallas import tpu as pltpu
from jax.sharding import PartitionSpec as P

MESH = pl.DeviceIdType.MESH
BF16, F32 = jnp.bfloat16, jnp.float32
D, PR, TOK = 4096, 64, 64
NT = (((1,), (1,)), ((), ()))
TN = (((0,), (0,)), ((), ()))
COLS, AHEAD = 2048, 2
SPLIT = D // COLS
PIECES = 4 * SPLIT
FORWARD = 6


def kernel(lens_hbm, acts, og, wi, wo, q, out,
           abuf, gbuf, wib, wob, xacc, gacc, pscr, pown, psend, pbuf, usend, ubuf, uf, qbuf, ssend, sbuf,
           lens, ld_sem, w_sem, q_ssem, q_rsem, c_ssem, c_rsem, e_ssem, e_rsem, s_ssem, s_rsem):
    b, g = lax.axis_index("blk"), lax.axis_index("grp")
    z, xl, y = b // 8, (b // 4) % 2, b % 4
    xh, core = g // 2, g % 2

    def dev(z_, xl_, y_, xh_, c_):
        return (z_ * 8 + xl_ * 4 + y_, xh_ * 2 + c_)

    up, down, far = (y + 1) % 4, (y + 3) % 4, (y + 2) % 4
    y_up, y_down = dev(z, xl, up, xh, core), dev(z, xl, down, xh, core)
    peers = [((z + dz) % 4, (xl + dx) % 2, (core + dc) % 2)
             for dz in (2, 1, 3, 0) for dx in (1, 0) for dc in (0, 1) if (dz, dx, dc) != (0, 0, 0)]

    def peer(i):
        z_, xl_, c_ = peers[i]
        return dev(z_, xl_, y, xh, c_), (z_ * 2 + xl_) * 2 + c_

    def target(s):
        return (xh + 1 - s // 2) % 2, (core + (s + 1) // 2) % 2

    barrier = pltpu.get_barrier_semaphore()
    partners = [y_up, y_down] + [peer(i)[0] for i in range(15)]
    partners += [dev(z, xl, y, *target(s)) for s in range(2)]
    for p in partners:
        pl.semaphore_signal(barrier, inc=1, device_id=p, device_id_type=MESH)

    def load(i):
        xt, ct = target(i // SPLIT)
        rows = pl.ds((xt * 2 + ct) * 4, 4)
        cols = pl.ds(pl.multiple_of((i % SPLIT) * COLS, COLS), COLS)
        return (pltpu.make_async_copy(acts.at[rows, :, cols], abuf.at[i], ld_sem.at[i, 0]),
                pltpu.make_async_copy(og.at[rows, :, cols], gbuf.at[i], ld_sem.at[i, 1]))

    w_loads = [pltpu.make_async_copy(wi, wib.at[pl.ds(0, PR)], w_sem.at[0]),
               pltpu.make_async_copy(wo, wob, w_sem.at[1])]
    q_load = pltpu.make_async_copy(
        q.at[:, pl.ds(pl.multiple_of(core * 2048, 2048), 2048)], qbuf.at[y], w_sem.at[2])
    for c in w_loads:
        c.start(priority=1)
    for k in range(AHEAD):
        for c in load(k):
            c.start(priority=1)
    q_load.start(priority=1)
    l_load = pltpu.make_async_copy(lens_hbm, lens, w_sem.at[3])
    l_load.start()

    q_moves = [(y, 0, y_up), (y, 1, y_down), (y, 1, y_up), (y, 0, y_down), (down, 0, y_up), (up, 1, y_down)]

    def move_q(i):
        slot, h, to = q_moves[i]
        half = qbuf.at[slot, pl.ds(h * 32, 32)]
        return pltpu.make_async_remote_copy(
            src_ref=half, dst_ref=half, send_sem=q_ssem.at[i], recv_sem=q_rsem.at[slot, h],
            device_id=to, device_id_type=MESH)

    def wait_q(slot, h):
        half = qbuf.at[slot, pl.ds(h * 32, 32)]
        pltpu.make_async_remote_copy(
            src_ref=half, dst_ref=half, send_sem=q_ssem.at[0], recv_sem=q_rsem.at[slot, h],
            device_id=y_up, device_id_type=MESH).wait_recv()

    def send_part(s):
        return pltpu.make_async_remote_copy(
            src_ref=psend.at[s], dst_ref=pbuf.at[g], send_sem=c_ssem.at[s], recv_sem=c_rsem.at[g],
            device_id=dev(z, xl, y, *target(s)), device_id_type=MESH)

    for c in w_loads:
        c.wait()
    l_load.wait()
    wib[pl.ds(PR, PR)] = wib[pl.ds(0, PR)]
    pos = lax.broadcasted_iota(jnp.int32, (TOK, PR), 0) + g * TOK
    low = lax.broadcasted_iota(jnp.int32, (32, 128), 1) < PR

    def step(i, carry):
        s, k = i // SPLIT, i % SPLIT
        for c in load(i):
            c.wait()

        @pl.when(i + AHEAD < PIECES)
        def _():
            for c in load(i + AHEAD):
                c.start(priority=1)

        cols = pl.ds(pl.multiple_of(k * COLS, COLS), COLS)
        xp = lax.dot_general(
            abuf[i].reshape(4 * TOK, COLS), wib[:, cols], NT, preferred_element_type=F32)
        gp = lax.dot_general(
            gbuf[i].reshape(4 * TOK, COLS), wob[:, cols], NT, preferred_element_type=F32)

        @pl.when(k == 0)
        def _():
            xacc[...] = xp
            gacc[...] = gp

        @pl.when(k > 0)
        def _():
            xacc[...] += xp
            gacc[...] += gp

        @pl.when(i == 0)
        def _():
            q_load.wait()
            pl.semaphore_wait(barrier, len(partners))
            for j in range(4):
                move_q(j).start()

        @pl.when(k == SPLIT - 1)
        def _():
            xt, ct = target(s)
            for c in range(4):
                rows = pl.ds(c * TOK, TOK)
                left = jnp.where(pos < lens[(xt * 2 + ct) * 4 + c], gacc[rows], 0.0).astype(BF16)
                pscr[c] = lax.dot_general(
                    left, xacc[rows].astype(BF16), TN, preferred_element_type=F32)
                part = jnp.where(
                    low, pscr[c, pl.ds(0, 32, stride=2), :], pscr[c, pl.ds(1, 32, stride=2), :])
                pown[c] = part
                psend[s, c] = part.astype(BF16)

        @pl.when(jnp.logical_and(k == SPLIT - 1, s < 3))
        def _():
            send_part(s).start()

        @pl.when(i == FORWARD)
        def _():
            wait_q(down, 0)
            move_q(4).start()
            wait_q(up, 1)
            move_q(5).start()

        return carry

    lax.fori_loop(0, PIECES, step, 0)

    total = pown[...]
    for s in range(3):
        xt, ct = target(s)
        src = xt * 2 + ct
        pltpu.make_async_remote_copy(
            src_ref=psend.at[s], dst_ref=pbuf.at[src], send_sem=c_ssem.at[s],
            recv_sem=c_rsem.at[src], device_id=dev(z, xl, y, xt, ct), device_id_type=MESH).wait_recv()
        total = total + pbuf[src].astype(F32)
    square = jnp.sum(jnp.sum(total * total, axis=2, keepdims=True), axis=1, keepdims=True)
    unit = (total * lax.rsqrt(square * (1.0 / 4096) + 1e-6)).astype(BF16)
    usend[0] = unit[:, :16]
    usend[1] = unit[:, 16:]

    me = (z * 2 + xl) * 2 + core

    def send_u(i):
        return pltpu.make_async_remote_copy(
            src_ref=usend.at[peers[i][2]], dst_ref=ubuf.at[me], send_sem=e_ssem.at[0],
            recv_sem=e_rsem.at[0], device_id=peer(i)[0], device_id_type=MESH)

    for i in range(15):
        send_u(i).start()
    ubuf[me] = usend[core]

    for slot, h in ((down, 1), (up, 0), (far, 0), (far, 1)):
        wait_q(slot, h)
    fifteen = pl.ds(0, 15)
    pltpu.make_async_remote_copy(
        src_ref=ubuf.at[fifteen], dst_ref=ubuf.at[fifteen], send_sem=e_ssem.at[0],
        recv_sem=e_rsem.at[0], device_id=peer(0)[0], device_id_type=MESH).wait_recv()
    uf[...] = ubuf[...].astype(F32).reshape(1024, 128)
    left = jnp.concatenate(
        [uf[pl.ds(r, 64, stride=16), :].astype(BF16) for r in range(16)], axis=1)
    scores = lax.dot_general(left, qbuf[...].reshape(256, 2048), NT, preferred_element_type=F32)
    for o in range(16):
        ssend[o] = scores[4 * o:4 * o + 4]

    def send_s(i):
        to, o = peer(i)
        return pltpu.make_async_remote_copy(
            src_ref=ssend.at[o], dst_ref=sbuf.at[me], send_sem=s_ssem.at[0],
            recv_sem=s_rsem.at[0], device_id=to, device_id_type=MESH)

    for i in range(15):
        send_s(i).start()
    sbuf[me] = ssend[me]
    for i in range(3):
        send_part(i).wait_send()
    for i in range(6):
        move_q(i).wait_send()
    pltpu.make_async_remote_copy(
        src_ref=ubuf.at[fifteen], dst_ref=ubuf.at[fifteen], send_sem=e_ssem.at[0],
        recv_sem=e_rsem.at[0], device_id=peer(0)[0], device_id_type=MESH).wait_send()
    pltpu.make_async_remote_copy(
        src_ref=sbuf.at[fifteen], dst_ref=sbuf.at[fifteen], send_sem=s_ssem.at[0],
        recv_sem=s_rsem.at[0], device_id=peer(0)[0], device_id_type=MESH).wait_recv()
    for o in range(8):
        out[:, o * 256:(o + 1) * 256] = sbuf[2 * o] + sbuf[2 * o + 1]
    pltpu.make_async_remote_copy(
        src_ref=ssend.at[fifteen], dst_ref=sbuf.at[fifteen], send_sem=s_ssem.at[0],
        recv_sem=s_rsem.at[0], device_id=peer(0)[0], device_id_type=MESH).wait_send()


def on_device(acts, out_grads, proj_in, proj_out, lengths, queries):
    any_space = pl.BlockSpec(memory_space=pltpu.HBM)
    dma = pltpu.SemaphoreType.DMA
    return pl.pallas_call(
        kernel,
        name="scores",
        out_shape=pltpu.VMEM((4, 2048), F32),
        in_specs=[any_space] * 6,
        out_specs=pl.BlockSpec(memory_space=pltpu.VMEM),
        scratch_shapes=[
            pltpu.VMEM((PIECES, 4, TOK, COLS), BF16),
            pltpu.VMEM((PIECES, 4, TOK, COLS), BF16),
            pltpu.VMEM((2 * PR, D), BF16),
            pltpu.VMEM((PR, D), BF16),
            pltpu.VMEM((4 * TOK, 2 * PR), F32),
            pltpu.VMEM((4 * TOK, PR), F32),
            pltpu.VMEM((4, PR, 2 * PR), F32),
            pltpu.VMEM((4, 32, 128), F32),
            pltpu.VMEM((4, 4, 32, 128), BF16),
            pltpu.VMEM((4, 4, 32, 128), BF16),
            pltpu.VMEM((2, 4, 16, 128), BF16),
            pltpu.VMEM((16, 4, 16, 128), BF16),
            pltpu.VMEM((1024, 128), F32),
            pltpu.VMEM((4, 64, 2048), BF16),
            pltpu.VMEM((16, 4, 256), F32),
            pltpu.VMEM((16, 4, 256), F32),
            pltpu.SMEM((16,), jnp.int32), dma((PIECES, 2)), dma((4,)), dma((6,)), dma((4, 2)), dma((3,)), dma((4,)),
            dma((1,)), dma((1,)), dma((1,)), dma((1,)),
        ],
        compiler_params=pltpu.CompilerParams(
            collective_id=0, has_side_effects=True, vmem_limit_bytes=62*2**20),
    )(lengths, acts[0], out_grads[0], proj_in[0].T, proj_out[0].T, queries)


def solution(mesh):
    in_specs = (
        P(None, "blk", "grp", None),
        P(None, "blk", "grp", None),
        P(),
        P(),
        P("blk"),
        P("blk", None),
    )
    return jax.shard_map(
        on_device, mesh=mesh, in_specs=in_specs, out_specs=P(("blk", "grp"), None), check_vma=False
    )
```
